32 devices in a mesh: shift: 1, blk: 16 (over z, y, x), depth: 2 (over core).
Axes of the slice: x: 2, y: 2, z: 4, core: 2. Of those that a mesh axis runs over, the one named last changes fastest.
Arguments:
- density: bfloat16 [32, 32, 128, 128], P(('shift', 'blk')), may hold values from -1.1953125 to 1.1953125
- product_tasks: int32 [3, 16, 4, 128], P(None, ('shift', 'blk')), may hold values from 0 to 64, as said below
Outputs:
- square_blocks: bfloat16 [32, 32, 128, 128], P(('shift', 'blk'), 'depth')
The draws below stay inside these ranges and needn't reach their ends.
Inputs may be any that keep to these rules, and one draw needn't show every extreme that they name: `product_tasks`: for each panel r and offset t the first tasks are exactly the triples in which slot a of panel r holds block (i, j) of P with block row j in panel (r + t) mod 16, slot b of that panel holds block (j, k), and c is the slot of block (i, k) in block row i, where P's block pattern stores 32 distinct block columns in each block row, its own among them; each triple once; the rest are (0, 0, 64). Some panel and offset has exactly 128 triples.
All inputs are finite; a program needn't handle non-finite values.
Results may differ from the reference program's by a relative error of at most 0.001.
Values may be sent and summed in bfloat16 or wider, within the bound.
A program may use at most 64 MiB of HBM per device.

```python
import jax
import jax.numpy as jnp
from jax import lax

BS = 128
K = 32
RB_DEV = 2
NB = 32
WIN = 4
TASKS = 128
N_BLK = 16


def pattern_columns(key):
    total_rows = RB_DEV * N_BLK
    key_noise, key_pick = jax.random.split(jax.random.fold_in(key, 7))
    noise = jax.random.randint(key_noise, (total_rows, total_rows), 0, 1024)
    places = jnp.arange(total_rows, dtype=jnp.int32)
    distance = jnp.abs(places[None, :] - places[:, None])
    distance = jnp.minimum(distance, total_rows - distance)
    score = distance * 160 + noise
    score = jnp.where(distance == 0, -1, score)
    chosen = jax.random.randint(key_pick, (), 0, N_BLK)
    in_cluster = places // RB_DEV == chosen
    cluster_row = jnp.take(score, chosen * RB_DEV, axis=0)
    cluster_row = jnp.where(in_cluster, -1, cluster_row)
    score = jnp.where(in_cluster[:, None], cluster_row[None, :], score)
    ranked = (score + 1) * total_rows + places[None, :]
    _, columns = lax.top_k(-ranked, K)
    return columns.astype(jnp.int32)


def draw_product_tasks(key, part):
    columns = pattern_columns(key)
    slots = RB_DEV * K
    mine = columns.reshape(N_BLK, slots)
    devices = jnp.arange(N_BLK, dtype=jnp.int32)
    offsets = jnp.arange(WIN, dtype=jnp.int32)
    target_panel = (devices[:, None] + offsets[None, :]) % N_BLK
    in_panel = mine[:, None, :] // RB_DEV == target_panel[:, :, None]
    inner = jnp.arange(K, dtype=jnp.int32)
    second_slot = (mine % RB_DEV)[:, :, None] * K + inner[None, None, :]
    second_column = jnp.take(columns, mine, axis=0)
    row_columns = columns.reshape(N_BLK, RB_DEV, K)
    row_local = jnp.arange(slots, dtype=jnp.int32) // K
    first_columns = row_columns[:, row_local, :]
    match = second_column[:, :, :, None] == first_columns[:, :, None, :]
    found = jnp.any(match, axis=-1)
    where_found = jnp.argmax(match.astype(jnp.int32), axis=-1).astype(jnp.int32)
    result_slot = row_local[None, :, None] * K + where_found
    first_slot = jnp.broadcast_to(jnp.arange(slots, dtype=jnp.int32)[None, :, None], (N_BLK, slots, K))
    valid = in_panel[:, :, :, None] & found[:, None, :, :]
    valid = valid.reshape(N_BLK, WIN, slots * K)
    position = jnp.cumsum(valid.astype(jnp.int32), axis=-1) - 1
    target = jnp.where(valid, position, TASKS)
    dev_index = jnp.broadcast_to(devices[:, None, None], target.shape)
    off_index = jnp.broadcast_to(offsets[None, :, None], target.shape)
    outputs = []
    for source, filler in ((first_slot, 0), (second_slot, 0), (result_slot, slots)):
        values = jnp.broadcast_to(source.reshape(N_BLK, 1, slots * K), target.shape)
        holder = jnp.full((N_BLK, WIN, TASKS + 1), filler, jnp.int32)
        holder = holder.at[dev_index, off_index, target].set(values)
        holder = holder.at[:, :, TASKS].set(filler)
        outputs.append(holder[:, :, :TASKS])
    return jnp.stack(outputs).astype(jnp.int32)


def steps_of(own_key, extent, shards, low, top_value):
    gain = 1.0
    for dim, blocks in shards:
        heights = jax.random.uniform(jax.random.fold_in(jax.random.fold_in(own_key, 6), dim), (blocks,), jnp.float32, low / len(shards), top_value / len(shards))
        gain = gain * jnp.repeat(jnp.exp(heights), extent[dim] // blocks).reshape((-1,) + (1,) * (len(extent) - 1 - dim))
    return gain


def bell_draw(stream_key, dims, width, most, shards=(), kind=jnp.bfloat16):
    loudness = steps_of(stream_key, dims, shards, -0.22, 0.18) if shards else 1.0
    entries = jax.random.normal(stream_key, dims, jnp.float32) * width * loudness
    return jnp.minimum(jnp.maximum(entries, -most), most).astype(kind)


def setup_inputs(seed: int = 0, part: int = 0) -> dict:
    key_of = jax.random.split(jax.random.key(seed), 3)
    part_keys = jax.random.split(jax.random.fold_in(key_of[2], part), 3)
    return {
        "density": bell_draw(part_keys[0], (NB, K, BS, BS), 0.2, 1.1953125, ((0, 16),)),
        "product_tasks": draw_product_tasks(jax.random.fold_in(jax.random.fold_in(key_of[2], part), 71), part),
    }


def reference(density, product_tasks):
    slots = RB_DEV * K
    panels = density.reshape(N_BLK, slots, BS, BS)

    def one_device(index):
        mine = lax.dynamic_index_in_dim(panels, index, 0, keepdims=False)
        total = jnp.zeros((slots + 1, BS, BS), jnp.float32)
        for offset in range(WIN):
            other = (index + offset) % N_BLK
            panel = lax.dynamic_index_in_dim(panels, other.astype(jnp.int32), 0, keepdims=False)
            tasks = lax.dynamic_index_in_dim(product_tasks[:, :, offset], index, 1, keepdims=False)
            first = jnp.take(mine, tasks[0], axis=0).astype(jnp.float32)
            second = jnp.take(panel, tasks[1], axis=0).astype(jnp.float32)
            products = jnp.einsum("nij,njk->nik", first, second)
            total = total + jax.ops.segment_sum(products, tasks[2], num_segments=slots + 1)
        return total[:slots].astype(jnp.bfloat16)

    result = lax.map(one_device, jnp.arange(N_BLK, dtype=jnp.int32))
    return result.reshape(N_BLK * RB_DEV, K, BS, BS)
```

```python
import functools

import jax
import jax.numpy as jnp
from jax import lax
from jax.experimental import pallas as pl
from jax.experimental.pallas import tpu as pltpu
from jax.sharding import PartitionSpec as P

MESH = pl.DeviceIdType.MESH
GROUP = 4
PASS = 0

OWN = {
    (0, 0): [(-1, 0, PASS)],
    (0, 1): [(-1, 0, PASS)],
    (1, 0): [(0, 0, 1), (-1, 1, PASS)],
    (1, 1): [(0, 0, 1), (-1, 1, PASS)],
    (2, 0): [(0, 0, 2), (-1, 2, PASS)],
    (2, 1): [(0, 0, 2), (0, 3, PASS)],
    (3, 0): [(0, 2, 1), (0, 1, 2)],
    (3, 1): [(0, 2, 1), (0, 1, 2)],
}
FIRST = {
    (0, 0): [(PASS, [(0, 1, 3), (0, 2, 2)]), (1, []), (2, [(0, 1, 1)])],
    (0, 1): [(PASS, [(0, 1, 3), (0, 2, 2)]), (1, [(0, 2, PASS)]), (2, [])],
    (1, 0): [(PASS, [(0, 3, 2)]), (2, []), (3, [(0, 3, 1)])],
    (1, 1): [(PASS, [(0, 3, 2)]), (2, [(0, 0, 3)]), (3, [])],
    (2, 0): [(PASS, [(0, 3, 3)]), (1, [(0, 0, 3)]), (2, [])],
    (2, 1): [(1, []), (2, [(0, 3, 1)]), (PASS, [(-1, 2, 3)])],
    (3, 0): [(2, [(0, 2, 3)])],
    (3, 1): [(PASS, [(-1, 3, 3), (0, 1, 1)]), (2, [])],
}
LAST = {
    (0, 0): [3],
    (0, 1): [3],
    (1, 0): [1],
    (1, 1): [1],
    (2, 0): [3],
    (2, 1): [3],
    (3, 0): [1, 3],
    (3, 1): [1, 3],
}


def kernel(n, density, tasks, out, *scratch):
    rows, slots, size = density.shape[0], density.shape[1], density.shape[2]
    window, count = tasks.shape[2], tasks.shape[3]
    win = scratch[:window]
    relay, lines, table, spots, send, got, give, take, local = scratch[window:]
    stored = rows * slots
    half = slots
    chunks = got.shape[1]
    part = half // chunks
    me = lax.axis_index("blk")
    h = lax.axis_index("depth")
    q = me % GROUP
    base = me - q

    def place(step, spot):
        return (base + step * GROUP + n + spot) % n

    def there(step, spot):
        return {"blk": place(step, spot)}

    partner = {"depth": 1 - h}
    barrier = pltpu.get_barrier_semaphore()
    greeted = [
        partner,
        {"blk": base + (q ^ 1)},
        {"blk": base + (q ^ 2)},
        {"blk": (me + GROUP) % n},
        {"blk": (me + n - GROUP) % n},
    ]
    for other in greeted:
        pl.semaphore_signal(barrier, inc=1, device_id=other, device_id_type=MESH)
    pl.semaphore_wait(barrier, len(greeted))

    def held(buffer, side, k, length):
        if buffer == PASS:
            return relay.at[pl.ds(k * part, length)]
        return win[buffer].at[pl.ds(side * half + k * part, length)]

    def remote(source, target, lane, k, length=part):
        step, spot, buffer = target
        return pltpu.make_async_remote_copy(
            src_ref=source,
            dst_ref=held(buffer, h, k, length),
            send_sem=send.at[lane],
            recv_sem=got.at[buffer, k],
            device_id=there(step, spot),
            device_id_type=MESH,
        )

    def passed(buffer, side, k, length=part):
        return pltpu.make_async_remote_copy(
            src_ref=held(buffer, side, k, length),
            dst_ref=held(buffer, side, k, length),
            send_sem=give.at[buffer],
            recv_sem=take.at[buffer],
            device_id=partner,
            device_id_type=MESH,
        )

    def roles(emit):
        for role in OWN:

            @pl.when(jnp.logical_and(q == role[0], h == role[1]))
            def _(role=role):
                emit(role)

    def emit_own(role):
        side = role[1]

        def push(k, _):
            source = density.at[side, pl.ds(k * part, part)]
            for lane, target in enumerate(OWN[role]):
                remote(source, target, lane, k).start()
            return 0

        lax.fori_loop(0, chunks, push, 0)

    roles(emit_own)

    mine = [
        pltpu.make_async_copy(density.at[r], win[0].at[pl.ds(r * slots, slots)], local.at[r])
        for r in range(rows)
    ]
    for copy in mine:
        copy.start()
    for t in range(window):
        win[t][stored] = jnp.zeros((size, size), density.dtype)

    mine_slots = out.shape[1]
    entries = rows * mine_slots * rows
    entry = lax.broadcasted_iota(jnp.int32, (entries, count), 0)
    column = lax.broadcasted_iota(jnp.int32, (entries, count), 1)
    entry_row = entry // (mine_slots * rows)
    entry_slot = entry // rows % mine_slots
    entry_inner = entry % rows
    wanted = entry_row * slots + h * mine_slots + entry_slot
    found = jnp.zeros((entries, count), jnp.int32)
    for t in range(window):
        first = jnp.broadcast_to(tasks[0, 0, t : t + 1, :], (entries, count))
        second = jnp.broadcast_to(tasks[1, 0, t : t + 1, :], (entries, count))
        result = jnp.broadcast_to(tasks[2, 0, t : t + 1, :], (entries, count))
        inner_ok = second // slots == entry_inner
        hit = jnp.logical_and(inner_ok, result == wanted)
        spot = jnp.max(jnp.where(hit, second, -1), axis=1, keepdims=True)
        spot = jnp.where(spot < 0, stored, spot)
        hit_row = jnp.logical_and(inner_ok, result // slots == entry_row)
        line = jnp.max(jnp.where(hit_row, first, 0), axis=1, keepdims=True)
        found = jnp.where(column == t, spot, found)
        found = jnp.where(column == window + t, line, found)
    table[...] = found
    fetch = pltpu.make_async_copy(table, spots, local.at[rows])
    fetch.start()
    fetch.wait()
    for copy in mine:
        copy.wait()

    for r in range(rows):
        for t in range(window):
            for j in range(rows):
                spot = spots[r * mine_slots * rows + j, window + t]
                at = (t * rows + j) * size
                lines[r, :, at : at + size] = win[0][spot]

    def emit_flow(role):
        side = role[1]

        def arrive(k, buffer, onward, lane):
            remote(held(buffer, side, k, part), (0, role[0], buffer), 0, k).wait_recv()
            for target in onward:
                remote(held(buffer, side, k, part), target, lane, k).start()
                lane += 1
            if buffer != PASS:
                passed(buffer, side, k).start()
            return lane

        def early(k, _):
            lane = len(OWN[role])
            for buffer, onward in FIRST[role]:
                lane = arrive(k, buffer, onward, lane)
            return 0

        def late(k, _):
            for buffer in LAST[role]:
                arrive(k, buffer, [], 0)
            return 0

        lax.fori_loop(0, chunks, early, 0)
        lax.fori_loop(0, chunks, late, 0)
        sent = len(OWN[role]) + sum(len(onward) for _, onward in FIRST[role])
        for lane in range(sent):
            remote(held(PASS, side, 0, half), (0, role[0], PASS), lane, 0, half).wait_send()

    roles(emit_flow)
    for t in range(1, window):
        passed(t, 1 - h, 0, half).wait_recv()
        passed(t, h, 0, half).wait_send()

    pair = 2
    for r in range(rows):

        def multiply(m, _, r=r):
            columns = []
            for s in range(pair):
                at = (r * mine_slots + m * pair + s) * rows
                blocks = [win[t][spots[at + j, t]] for t in range(window) for j in range(rows)]
                columns.append(jnp.concatenate(blocks, axis=0))
            right = jnp.concatenate(columns, axis=1)
            value = jnp.dot(lines[r], right, preferred_element_type=jnp.float32)
            for s in range(pair):
                out[r, m * pair + s] = value[:, s * size : (s + 1) * size].astype(out.dtype)
            return 0

        lax.fori_loop(0, mine_slots // pair, multiply, 0)


def solution(mesh):
    n = mesh.shape["blk"]
    layers = mesh.shape["depth"]

    def body(density, product_tasks):
        rows, slots, size = density.shape[0], density.shape[1], density.shape[2]
        window, count = product_tasks.shape[2], product_tasks.shape[3]
        stored = rows * slots
        mine_slots = slots // layers
        entries = rows * mine_slots * rows
        chunks = 8
        lanes = max(len(OWN[r]) + sum(len(o) for _, o in FIRST[r]) for r in OWN)
        return pl.pallas_call(
            functools.partial(kernel, n),
            out_shape=jax.ShapeDtypeStruct((rows, mine_slots, size, size), density.dtype),
            in_specs=[
                pl.BlockSpec(memory_space=pl.ANY),
                pl.BlockSpec(memory_space=pltpu.VMEM),
            ],
            out_specs=pl.BlockSpec(memory_space=pltpu.VMEM),
            scratch_shapes=[
                *[pltpu.VMEM((stored + 1, size, size), density.dtype)] * window,
                pltpu.VMEM((slots, size, size), density.dtype),
                pltpu.VMEM((rows, size, window * rows * size), density.dtype),
                pltpu.VMEM((entries, count), jnp.int32),
                pltpu.SMEM((entries, count), jnp.int32),
                pltpu.SemaphoreType.DMA((lanes,)),
                pltpu.SemaphoreType.DMA((window, chunks)),
                pltpu.SemaphoreType.DMA((window,)),
                pltpu.SemaphoreType.DMA((window,)),
                pltpu.SemaphoreType.DMA((rows + 1,)),
            ],
            compiler_params=pltpu.CompilerParams(collective_id=0, has_side_effects=True),
        )(density, product_tasks)

    placed = (P(("shift", "blk"), None, None, None), P(None, ("shift", "blk"), None, None))
    return jax.shard_map(
        body,
        mesh=mesh,
        in_specs=placed,
        out_specs=P(("shift", "blk"), "depth", None, None),
        check_vma=False,
    )
```

```python
import functools
import heapq

import jax
import jax.numpy as jnp
from jax import lax
from jax.experimental import pallas as pl
from jax.experimental.pallas import tpu as pltpu
from jax.sharding import PartitionSpec as P

MESH = pl.DeviceIdType.MESH
GROUP = 4

TREES = {
    (0, 0): [((0, 0), (0, 1)), ((0, 1), (-1, 1)), ((-1, 1), (-1, 3)), ((0, 0), (-1, 0)), ((-1, 0), (-1, 2))],
    (0, 1): [((0, 0), (0, 2)), ((0, 2), (-1, 2)), ((-1, 2), (-1, 3)), ((0, 0), (-1, 0)), ((-1, 0), (-1, 1))],
    (1, 0): [((0, 1), (0, 0)), ((0, 1), (0, 3)), ((0, 3), (-1, 3)), ((-1, 3), (-1, 2))],
    (1, 1): [((0, 1), (0, 0)), ((0, 1), (-1, 1)), ((0, 0), (0, 2)), ((0, 2), (-1, 2)), ((-1, 1), (-1, 3))],
    (2, 0): [((0, 2), (0, 0)), ((0, 2), (-1, 2)), ((0, 0), (0, 1)), ((-1, 2), (-1, 3))],
    (2, 1): [((0, 2), (0, 3)), ((0, 2), (0, 0)), ((0, 3), (0, 1)), ((0, 3), (-1, 3))],
    (3, 0): [((0, 3), (0, 2)), ((0, 3), (0, 1)), ((0, 2), (0, 0))],
    (3, 1): [((0, 3), (0, 1)), ((0, 3), (0, 2)), ((0, 1), (0, 0))],
}
LINK_TIME = 1.41 / 65536
HOP_TIME = 1.6
SLACK = 3.0


def buffers():
    found, used = {}, {}
    for (panel, tree), edges in TREES.items():
        for _, (step, spot) in edges:
            offset = panel - spot - GROUP * step
            if not 0 < offset < GROUP:
                offset = used.get((spot, tree), GROUP)
                used[spot, tree] = offset + 1
            found[panel, tree, (step, spot)] = offset
    return found, max(used.values())


def make_plan(chunks, chunk_bytes):
    filled, total = buffers()

    def hop(panel, tree, source, target):
        return (target[0] - source[0], target[1], filled[panel, tree, target])

    first = []
    for (panel, tree), edges in TREES.items():
        for source, target in edges:
            if source == (0, panel):
                leaf = all(after != target for after, _ in edges)
                first += [(leaf, k, panel, tree, source, target) for k in range(chunks)]
    first.sort(key=lambda item: item[:2])
    own, seen = {q: [] for q in range(GROUP)}, {q: [] for q in range(GROUP)}
    queue, free = [], {}
    for serial, (_, k, panel, tree, source, target) in enumerate(first):
        heapq.heappush(queue, (0.0, serial, panel, tree, k, source, target))
        own[panel].append((tree, k, hop(panel, tree, source, target)))
    serial = len(first)
    while queue:
        now, _, panel, tree, k, source, target = heapq.heappop(queue)
        link = (source[1], target[1], target[0] - source[0])
        free[link] = max(now, free.get(link, 0.0)) + chunk_bytes * LINK_TIME
        done = free[link] + HOP_TIME
        onward = []
        for after, further in TREES[panel, tree]:
            if after == target:
                heapq.heappush(queue, (done, serial, panel, tree, k, after, further))
                serial += 1
                onward.append(hop(panel, tree, after, further))
        seen[target[1]].append((done, filled[panel, tree, target], (tree, k, onward)))
    events, tails = {}, {}
    for spot, arrivals in seen.items():
        end = max(done for done, _, _ in arrivals)
        mixed, tails[spot] = list(arrivals), []
        for t in range(1, GROUP):
            ready = max(done for done, buffer, _ in arrivals if buffer == t) + SLACK
            if ready < end - SLACK:
                mixed.append((ready, t, None))
            else:
                tails[spot].append(t)
        events[spot] = sorted(mixed, key=lambda event: event[0])
    return own, events, tails, total


def kernel(n, own, events, tails, density, tasks_in, out, *scratch):
    rows, slots, size = density.shape[0], density.shape[1], density.shape[2]
    window, count = tasks_in.shape[2], tasks_in.shape[3]
    win = scratch[:window]
    relay, lines, total, tasks, table, spots, send, got, give, take, local = scratch[window:]
    stored = rows * slots
    half = slots
    trees, chunks = got.shape[1], got.shape[2]
    part = half // (trees * chunks)
    me = lax.axis_index("blk")
    h = lax.axis_index("depth")
    q = me % GROUP
    base = me - q

    def place(step, spot):
        return (base + step * GROUP + n + spot) % n

    def there(step, spot):
        return {"blk": place(step, spot)}

    partner = {"depth": 1 - h}
    barrier = pltpu.get_barrier_semaphore()
    greeted = [
        partner,
        {"blk": base + (q ^ 1)},
        {"blk": base + (q ^ 2)},
        {"blk": (me + GROUP) % n},
        {"blk": (me + n - GROUP) % n},
    ]
    for other in greeted:
        pl.semaphore_signal(barrier, inc=1, device_id=other, device_id_type=MESH)
    pl.semaphore_wait(barrier, len(greeted))

    def held(buffer, side, at, length):
        if buffer >= window:
            return relay.at[pl.ds((buffer - window) * half + at, length)]
        return win[buffer].at[pl.ds(side * half + at, length)]

    def start(source, tree, k, hop):
        step, spot, buffer = hop
        at = (tree * chunks + k) * part
        pltpu.make_async_remote_copy(
            src_ref=source,
            dst_ref=held(buffer, h, at, part),
            send_sem=send.at[0],
            recv_sem=got.at[buffer, tree, k],
            device_id=there(step, spot),
            device_id_type=MESH,
        ).start()

    def passed(buffer, side, at, length):
        return pltpu.make_async_remote_copy(
            src_ref=held(buffer, side, at, length),
            dst_ref=held(buffer, side, at, length),
            send_sem=give.at[buffer],
            recv_sem=take.at[buffer],
            device_id=partner,
            device_id_type=MESH,
        )

    def places(emit):
        for spot in range(GROUP):

            @pl.when(q == spot)
            def _(spot=spot):
                emit(spot)

    def emit_own(spot):
        for tree, k, hop in own[spot]:
            at = (tree * chunks + k) * part
            start(density.at[h, pl.ds(at, part)], tree, k, hop)

    places(emit_own)

    mine = [
        pltpu.make_async_copy(density.at[r], win[0].at[pl.ds(r * slots, slots)], local.at[r])
        for r in range(rows)
    ]
    listed = pltpu.make_async_copy(tasks_in, tasks, local.at[rows])
    listed.start()
    for copy in mine:
        copy.start()
    for t in range(window):
        win[t][stored] = jnp.zeros((size, size), density.dtype)

    listed.wait()
    mine_slots = out.shape[1]
    entries = rows * mine_slots * rows
    entry = lax.broadcasted_iota(jnp.int32, (entries, count), 0)
    column = lax.broadcasted_iota(jnp.int32, (entries, count), 1)
    entry_row = entry // (mine_slots * rows)
    entry_slot = entry // rows % mine_slots
    entry_inner = entry % rows
    wanted = entry_row * slots + h * mine_slots + entry_slot
    found = jnp.zeros((entries, count), jnp.int32)
    for t in range(window):
        first = jnp.broadcast_to(tasks[0, 0, t : t + 1, :], (entries, count))
        second = jnp.broadcast_to(tasks[1, 0, t : t + 1, :], (entries, count))
        result = jnp.broadcast_to(tasks[2, 0, t : t + 1, :], (entries, count))
        inner_ok = second // slots == entry_inner
        hit = jnp.logical_and(inner_ok, result == wanted)
        spot = jnp.max(jnp.where(hit, second, -1), axis=1, keepdims=True)
        spot = jnp.where(spot < 0, stored, spot)
        hit_row = jnp.logical_and(inner_ok, result // slots == entry_row)
        line = jnp.max(jnp.where(hit_row, first, 0), axis=1, keepdims=True)
        found = jnp.where(column == t, spot, found)
        found = jnp.where(column == window + t, line, found)
    table[...] = found
    fetch = pltpu.make_async_copy(table, spots, local.at[rows])
    fetch.start()
    fetch.wait()
    for copy in mine:
        copy.wait()

    for r in range(rows):
        for t in range(window):
            for j in range(rows):
                spot = spots[r * mine_slots * rows + j, window + t]
                at = (t * rows + j) * size
                lines[r, :, at : at + size] = win[0][spot]

    pair = 2

    def multiply(offsets, begin, end):
        for t in offsets:
            if t > 0:
                passed(t, 1 - h, 0, half).wait_recv()
                passed(t, h, 0, half).wait_send()
        width = rows * size
        for r in range(rows):

            def step(m, _, r=r):
                columns = []
                for s in range(pair):
                    at = (r * mine_slots + m * pair + s) * rows
                    blocks = [win[t][spots[at + j, t]] for t in offsets for j in range(rows)]
                    columns.append(jnp.concatenate(blocks, axis=0))
                right = jnp.concatenate(columns, axis=1)
                left = jnp.concatenate([lines[r, :, t * width : (t + 1) * width] for t in offsets], axis=1)
                value = jnp.dot(left, right, preferred_element_type=jnp.float32)
                if not begin:
                    value = value + total[r, m]
                if not end:
                    total[r, m] = value
                    return 0
                for s in range(pair):
                    out[r, m * pair + s] = value[:, s * size : (s + 1) * size].astype(out.dtype)
                return 0

            lax.fori_loop(0, mine_slots // pair, step, 0)

    def emit_flow(spot):
        sent = len(own[spot])
        for _, buffer, event in events[spot]:
            if event is None:
                multiply([buffer], False, False)
                continue
            tree, k, onward = event
            at = (tree * chunks + k) * part
            chunk = held(buffer, h, at, part)
            pltpu.make_async_copy(chunk, chunk, got.at[buffer, tree, k]).wait()
            for hop in onward:
                start(chunk, tree, k, hop)
            sent += len(onward)
            if buffer < window:
                passed(buffer, h, at, part).start()
        multiply(tails[spot], False, True)
        left = sent * part
        while left > 0:
            length = min(left, half)
            chunk = held(window, h, 0, length)
            pltpu.make_async_copy(chunk, chunk, send.at[0]).wait()
            left -= length

    multiply([0], True, False)
    places(emit_flow)


def solution(mesh):
    n = mesh.shape["blk"]
    layers = mesh.shape["depth"]

    def body(density, product_tasks):
        rows, slots, size = density.shape[0], density.shape[1], density.shape[2]
        window, count = product_tasks.shape[2], product_tasks.shape[3]
        stored = rows * slots
        mine_slots = slots // layers
        entries = rows * mine_slots * rows
        chunks = 8
        trees = 2
        chunk_bytes = slots // (trees * chunks) * size * size * density.dtype.itemsize
        own, events, tails, total = make_plan(chunks, chunk_bytes)
        return pl.pallas_call(
            functools.partial(kernel, n, own, events, tails),
            out_shape=jax.ShapeDtypeStruct((rows, mine_slots, size, size), density.dtype),
            in_specs=[
                pl.BlockSpec(memory_space=pltpu.HBM),
                pl.BlockSpec(memory_space=pltpu.HBM),
            ],
            out_specs=pl.BlockSpec(memory_space=pltpu.VMEM),
            scratch_shapes=[
                *[pltpu.VMEM((stored + 1, size, size), density.dtype)] * window,
                pltpu.VMEM(((total - window) * slots, size, size), density.dtype),
                pltpu.VMEM((rows, size, window * rows * size), density.dtype),
                pltpu.VMEM((rows, mine_slots // 2, size, 2 * size), jnp.float32),
                pltpu.VMEM(product_tasks.shape, jnp.int32),
                pltpu.VMEM((entries, count), jnp.int32),
                pltpu.SMEM((entries, count), jnp.int32),
                pltpu.SemaphoreType.DMA((1,)),
                pltpu.SemaphoreType.DMA((total, trees, chunks)),
                pltpu.SemaphoreType.DMA((window,)),
                pltpu.SemaphoreType.DMA((window,)),
                pltpu.SemaphoreType.DMA((rows + 1,)),
            ],
            compiler_params=pltpu.CompilerParams(collective_id=0, has_side_effects=True, vmem_limit_bytes=24 << 20),
        )(density, product_tasks)

    placed = (P(("shift", "blk"), None, None, None), P(None, ("shift", "blk"), None, None))
    return jax.shard_map(
        body,
        mesh=mesh,
        in_specs=placed,
        out_specs=P(("shift", "blk"), "depth", None, None),
        check_vma=False,
    )
```

```python
import functools
import heapq

import jax
import jax.numpy as jnp
from jax import lax
from jax.experimental import pallas as pl
from jax.experimental.pallas import tpu as pltpu
from jax.sharding import PartitionSpec as P

MESH = pl.DeviceIdType.MESH
GROUP = 4

TREES = {
    (0, 0): [((0, 0), (0, 1)), ((0, 1), (-1, 1)), ((-1, 1), (-1, 3)), ((0, 0), (-1, 0)), ((-1, 0), (-1, 2))],
    (0, 1): [((0, 0), (0, 2)), ((0, 2), (-1, 2)), ((-1, 2), (-1, 3)), ((0, 0), (-1, 0)), ((-1, 0), (-1, 1))],
    (1, 0): [((0, 1), (0, 0)), ((0, 1), (0, 3)), ((0, 3), (-1, 3)), ((-1, 3), (-1, 2))],
    (1, 1): [((0, 1), (0, 0)), ((0, 1), (-1, 1)), ((0, 0), (0, 2)), ((0, 2), (-1, 2)), ((-1, 1), (-1, 3))],
    (2, 0): [((0, 2), (0, 0)), ((0, 2), (-1, 2)), ((0, 0), (0, 1)), ((-1, 2), (-1, 3))],
    (2, 1): [((0, 2), (0, 3)), ((0, 2), (0, 0)), ((0, 3), (0, 1)), ((0, 3), (-1, 3))],
    (3, 0): [((0, 3), (0, 2)), ((0, 3), (0, 1)), ((0, 2), (0, 0))],
    (3, 1): [((0, 3), (0, 1)), ((0, 3), (0, 2)), ((0, 1), (0, 0))],
}
LINK_TIME = 1.41 / 65536
HOP_TIME = 1.6
SLACK = 3.0


def buffers():
    found, used = {}, {}
    for (panel, tree), edges in TREES.items():
        for _, (step, spot) in edges:
            offset = panel - spot - GROUP * step
            if not 0 < offset < GROUP:
                offset = used.get((spot, tree), GROUP)
                used[spot, tree] = offset + 1
            found[panel, tree, (step, spot)] = offset
    return found, max(used.values())


def make_plan(chunks, chunk_bytes):
    filled, total = buffers()

    def hop(panel, tree, source, target):
        return (target[0] - source[0], target[1], filled[panel, tree, target])

    first = []
    for (panel, tree), edges in TREES.items():
        for source, target in edges:
            if source == (0, panel):
                leaf = all(after != target for after, _ in edges)
                first += [(leaf, k, panel, tree, source, target) for k in range(chunks)]
    first.sort(key=lambda item: item[:2])
    own, seen = {q: [] for q in range(GROUP)}, {q: [] for q in range(GROUP)}
    queue, free = [], {}
    for serial, (_, k, panel, tree, source, target) in enumerate(first):
        heapq.heappush(queue, (0.0, serial, panel, tree, k, source, target))
        own[panel].append((tree, k, hop(panel, tree, source, target)))
    serial = len(first)
    while queue:
        now, _, panel, tree, k, source, target = heapq.heappop(queue)
        link = (source[1], target[1], target[0] - source[0])
        free[link] = max(now, free.get(link, 0.0)) + chunk_bytes * LINK_TIME
        done = free[link] + HOP_TIME
        onward = []
        for after, further in TREES[panel, tree]:
            if after == target:
                heapq.heappush(queue, (done, serial, panel, tree, k, after, further))
                serial += 1
                onward.append(hop(panel, tree, after, further))
        seen[target[1]].append((done, filled[panel, tree, target], (tree, k, onward)))
    events, tails = {}, {}
    for spot, arrivals in seen.items():
        end = max(done for done, _, _ in arrivals)
        mixed, tails[spot] = list(arrivals), []
        for t in range(1, GROUP):
            ready = max(done for done, buffer, _ in arrivals if buffer == t) + SLACK
            if ready < end - SLACK:
                mixed.append((ready, t, None))
            else:
                tails[spot].append(t)
        events[spot] = sorted(mixed, key=lambda event: event[0])
    return own, events, tails, total


def kernel(n, own, events, tails, density, tasks_in, out, *scratch):
    rows, slots, size = density.shape[0], density.shape[1], density.shape[2]
    window, count = tasks_in.shape[2], tasks_in.shape[3]
    win = scratch[:window]
    relay, lines, total, tasks, table, spots, send, got, give, take, local = scratch[window:]
    stored = rows * slots
    half = slots
    trees, chunks = got.shape[1], got.shape[2]
    part = half // (trees * chunks)
    me = lax.axis_index("blk")
    h = lax.axis_index("depth")
    q = me % GROUP
    base = me - q

    def place(step, spot):
        return (base + step * GROUP + n + spot) % n

    def there(step, spot):
        return {"blk": place(step, spot)}

    partner = {"depth": 1 - h}
    barrier = pltpu.get_barrier_semaphore()
    greeted = [
        partner,
        {"blk": base + (q ^ 1)},
        {"blk": base + (q ^ 2)},
        {"blk": (me + GROUP) % n},
        {"blk": (me + n - GROUP) % n},
    ]
    for other in greeted:
        pl.semaphore_signal(barrier, inc=1, device_id=other, device_id_type=MESH)
    pl.semaphore_wait(barrier, len(greeted))

    def held(buffer, side, at, length):
        if buffer >= window:
            return relay.at[pl.ds((buffer - window) * half + at, length)]
        return win[buffer].at[pl.ds(side * half + at, length)]

    def start(source, tree, k, hop):
        step, spot, buffer = hop
        at = (tree * chunks + k) * part
        pltpu.make_async_remote_copy(
            src_ref=source,
            dst_ref=held(buffer, h, at, part),
            send_sem=send.at[0],
            recv_sem=got.at[buffer, tree, k],
            device_id=there(step, spot),
            device_id_type=MESH,
        ).start()

    def passed(buffer, side, at, length):
        return pltpu.make_async_remote_copy(
            src_ref=held(buffer, side, at, length),
            dst_ref=held(buffer, side, at, length),
            send_sem=give.at[buffer],
            recv_sem=take.at[buffer],
            device_id=partner,
            device_id_type=MESH,
        )

    def places(emit):
        for spot in range(GROUP):

            @pl.when(q == spot)
            def _(spot=spot):
                emit(spot)

    def emit_own(spot):
        for tree, k, hop in own[spot]:
            at = (tree * chunks + k) * part
            start(density.at[h, pl.ds(at, part)], tree, k, hop)

    places(emit_own)

    mine = [
        pltpu.make_async_copy(density.at[r], win[0].at[pl.ds(r * slots, slots)], local.at[r])
        for r in range(rows)
    ]
    listed = pltpu.make_async_copy(tasks_in, tasks, local.at[rows])
    listed.start()
    for copy in mine:
        copy.start()
    for t in range(window):
        win[t][stored] = jnp.zeros((size, size), density.dtype)

    listed.wait()
    mine_slots = out.shape[1]
    entries = rows * mine_slots * rows
    entry = lax.broadcasted_iota(jnp.int32, (entries, count), 0)
    column = lax.broadcasted_iota(jnp.int32, (entries, count), 1)
    entry_row = entry // (mine_slots * rows)
    entry_slot = entry // rows % mine_slots
    entry_inner = entry % rows
    wanted = entry_row * slots + h * mine_slots + entry_slot
    found = jnp.zeros((entries, count), jnp.int32)
    for t in range(window):
        first = jnp.broadcast_to(tasks[0, 0, t : t + 1, :], (entries, count))
        second = jnp.broadcast_to(tasks[1, 0, t : t + 1, :], (entries, count))
        result = jnp.broadcast_to(tasks[2, 0, t : t + 1, :], (entries, count))
        inner_ok = second // slots == entry_inner
        hit = jnp.logical_and(inner_ok, result == wanted)
        spot = jnp.max(jnp.where(hit, second, -1), axis=1, keepdims=True)
        spot = jnp.where(spot < 0, stored, spot)
        hit_row = jnp.logical_and(inner_ok, result // slots == entry_row)
        line = jnp.max(jnp.where(hit_row, first, 0), axis=1, keepdims=True)
        found = jnp.where(column == t, spot, found)
        found = jnp.where(column == window + t, line, found)
    table[...] = found
    fetch = pltpu.make_async_copy(table, spots, local.at[rows])
    fetch.start()
    fetch.wait()
    for copy in mine:
        copy.wait()

    for r in range(rows):
        for t in range(window):
            for j in range(rows):
                spot = spots[r * mine_slots * rows + j, window + t]
                at = (t * rows + j) * size
                lines[r, :, at : at + size] = win[0][spot]

    pair = 2

    def multiply(offsets, begin, end):
        for t in offsets:
            if t > 0:
                passed(t, 1 - h, 0, half).wait_recv()
                passed(t, h, 0, half).wait_send()
        width = rows * size
        for r in range(rows):

            def step(m, _, r=r):
                columns = []
                for s in range(pair):
                    at = (r * mine_slots + m * pair + s) * rows
                    blocks = [win[t][spots[at + j, t]] for t in offsets for j in range(rows)]
                    columns.append(jnp.concatenate(blocks, axis=0))
                right = jnp.concatenate(columns, axis=1)
                left = jnp.concatenate([lines[r, :, t * width : (t + 1) * width] for t in offsets], axis=1)
                value = jnp.dot(left, right, preferred_element_type=jnp.float32)
                if not begin:
                    value = value + total[r, m]
                if not end:
                    total[r, m] = value
                    return 0
                for s in range(pair):
                    out[r, m * pair + s] = value[:, s * size : (s + 1) * size].astype(out.dtype)
                return 0

            lax.fori_loop(0, mine_slots // pair, step, 0)

    def emit_flow(spot):
        sent = len(own[spot])
        for _, buffer, event in events[spot]:
            if event is None:
                multiply([buffer], False, False)
                continue
            tree, k, onward = event
            at = (tree * chunks + k) * part
            chunk = held(buffer, h, at, part)
            pltpu.make_async_copy(chunk, chunk, got.at[buffer, tree, k]).wait()
            for hop in onward:
                start(chunk, tree, k, hop)
            sent += len(onward)
            if buffer < window:
                passed(buffer, h, at, part).start()
        multiply(tails[spot], False, True)
        left = sent * part
        while left > 0:
            length = min(left, half)
            chunk = held(window, h, 0, length)
            pltpu.make_async_copy(chunk, chunk, send.at[0]).wait()
            left -= length

    multiply([0], True, False)
    places(emit_flow)


def solution(mesh):
    n = mesh.shape["blk"]
    layers = mesh.shape["depth"]

    def body(density, product_tasks):
        rows, slots, size = density.shape[0], density.shape[1], density.shape[2]
        window, count = product_tasks.shape[2], product_tasks.shape[3]
        stored = rows * slots
        mine_slots = slots // layers
        entries = rows * mine_slots * rows
        chunks = 8
        trees = 2
        chunk_bytes = slots // (trees * chunks) * size * size * density.dtype.itemsize
        own, events, tails, total = make_plan(chunks, chunk_bytes)
        density = pltpu.with_memory_space_constraint(density, pltpu.HBM)
        product_tasks = pltpu.with_memory_space_constraint(product_tasks, pltpu.HBM)
        return pl.pallas_call(
            functools.partial(kernel, n, own, events, tails),
            out_shape=jax.ShapeDtypeStruct((rows, mine_slots, size, size), density.dtype),
            in_specs=[
                pl.BlockSpec(memory_space=pltpu.HBM),
                pl.BlockSpec(memory_space=pltpu.HBM),
            ],
            out_specs=pl.BlockSpec(memory_space=pltpu.VMEM),
            scratch_shapes=[
                *[pltpu.VMEM((stored + 1, size, size), density.dtype)] * window,
                pltpu.VMEM(((total - window) * slots, size, size), density.dtype),
                pltpu.VMEM((rows, size, window * rows * size), density.dtype),
                pltpu.VMEM((rows, mine_slots // 2, size, 2 * size), jnp.float32),
                pltpu.VMEM(product_tasks.shape, jnp.int32),
                pltpu.VMEM((entries, count), jnp.int32),
                pltpu.SMEM((entries, count), jnp.int32),
                pltpu.SemaphoreType.DMA((1,)),
                pltpu.SemaphoreType.DMA((total, trees, chunks)),
                pltpu.SemaphoreType.DMA((window,)),
                pltpu.SemaphoreType.DMA((window,)),
                pltpu.SemaphoreType.DMA((rows + 1,)),
            ],
            compiler_params=pltpu.CompilerParams(collective_id=0, has_side_effects=True, vmem_limit_bytes=24 << 20),
        )(density, product_tasks)

    placed = (P(("shift", "blk"), None, None, None), P(None, ("shift", "blk"), None, None))
    return jax.shard_map(
        body,
        mesh=mesh,
        in_specs=placed,
        out_specs=P(("shift", "blk"), "depth", None, None),
        check_vma=False,
    )
```

```python
import functools
import heapq

import jax
import jax.numpy as jnp
from jax import lax
from jax.experimental import pallas as pl
from jax.experimental.pallas import tpu as pltpu
from jax.sharding import PartitionSpec as P

MESH = pl.DeviceIdType.MESH
GROUP = 4

TREES = {
    (0, 0): [((0, 0), (0, 1)), ((0, 1), (-1, 1)), ((-1, 1), (-1, 3)), ((0, 0), (-1, 0)), ((-1, 0), (-1, 2))],
    (0, 1): [((0, 0), (0, 2)), ((0, 2), (-1, 2)), ((-1, 2), (-1, 3)), ((0, 0), (-1, 0)), ((-1, 0), (-1, 1))],
    (1, 0): [((0, 1), (0, 0)), ((0, 1), (0, 3)), ((0, 3), (-1, 3)), ((-1, 3), (-1, 2))],
    (1, 1): [((0, 1), (0, 0)), ((0, 1), (-1, 1)), ((0, 0), (0, 2)), ((0, 2), (-1, 2)), ((-1, 1), (-1, 3))],
    (2, 0): [((0, 2), (0, 0)), ((0, 2), (-1, 2)), ((0, 0), (0, 1)), ((-1, 2), (-1, 3))],
    (2, 1): [((0, 2), (0, 3)), ((0, 2), (0, 0)), ((0, 3), (0, 1)), ((0, 3), (-1, 3))],
    (3, 0): [((0, 3), (0, 2)), ((0, 3), (0, 1)), ((0, 2), (0, 0))],
    (3, 1): [((0, 3), (0, 1)), ((0, 3), (0, 2)), ((0, 1), (0, 0))],
}
LINK_TIME = 1.41 / 65536
HOP_TIME = 1.6
SLACK = 3.0


def buffers():
    found, used = {}, {}
    for (panel, tree), edges in TREES.items():
        for _, (step, spot) in edges:
            offset = panel - spot - GROUP * step
            if not 0 < offset < GROUP:
                offset = used.get((spot, tree), GROUP)
                used[spot, tree] = offset + 1
            found[panel, tree, (step, spot)] = offset
    return found, max(used.values())


def make_plan(chunks, chunk_bytes):
    filled, total = buffers()

    def hop(panel, tree, source, target):
        return (target[0] - source[0], target[1], filled[panel, tree, target])

    first = []
    for (panel, tree), edges in TREES.items():
        for source, target in edges:
            if source == (0, panel):
                leaf = all(after != target for after, _ in edges)
                first += [(leaf, k, panel, tree, source, target) for k in range(chunks)]
    first.sort(key=lambda item: item[:2])
    own, seen = {q: [] for q in range(GROUP)}, {q: [] for q in range(GROUP)}
    queue, free = [], {}
    for serial, (_, k, panel, tree, source, target) in enumerate(first):
        heapq.heappush(queue, (0.0, serial, panel, tree, k, source, target))
        own[panel].append((tree, k, hop(panel, tree, source, target)))
    serial = len(first)
    while queue:
        now, _, panel, tree, k, source, target = heapq.heappop(queue)
        link = (source[1], target[1], target[0] - source[0])
        free[link] = max(now, free.get(link, 0.0)) + chunk_bytes * LINK_TIME
        done = free[link] + HOP_TIME
        onward = []
        for after, further in TREES[panel, tree]:
            if after == target:
                heapq.heappush(queue, (done, serial, panel, tree, k, after, further))
                serial += 1
                onward.append(hop(panel, tree, after, further))
        seen[target[1]].append((done, filled[panel, tree, target], (tree, k, onward)))
    events, tails = {}, {}
    for spot, arrivals in seen.items():
        end = max(done for done, _, _ in arrivals)
        mixed, tails[spot] = list(arrivals), []
        for t in range(1, GROUP):
            ready = max(done for done, buffer, _ in arrivals if buffer == t) + SLACK
            if ready < end - SLACK:
                mixed.append((ready, t, None))
            else:
                tails[spot].append(t)
        events[spot] = sorted(mixed, key=lambda event: event[0])
    return own, events, tails, total


def kernel(n, own, events, tails, density, tasks_in, out, *scratch):
    rows, slots, size = density.shape[0], density.shape[1], density.shape[2]
    window, count = tasks_in.shape[2], tasks_in.shape[3]
    win = scratch[:window]
    relay, lines, total, tasks, table, spots, send, got, give, take, local = scratch[window:]
    stored = rows * slots
    half = slots
    trees, chunks = got.shape[1], got.shape[2]
    part = half // (trees * chunks)
    me = lax.axis_index("blk")
    h = lax.axis_index("depth")
    q = me % GROUP
    base = me - q

    def place(step, spot):
        return (base + step * GROUP + n + spot) % n

    def there(step, spot):
        return {"blk": place(step, spot)}

    partner = {"depth": 1 - h}
    barrier = pltpu.get_barrier_semaphore()
    greeted = [
        partner,
        {"blk": base + (q ^ 1)},
        {"blk": base + (q ^ 2)},
        {"blk": (me + GROUP) % n},
        {"blk": (me + n - GROUP) % n},
    ]
    for other in greeted:
        pl.semaphore_signal(barrier, inc=1, device_id=other, device_id_type=MESH)
    pl.semaphore_wait(barrier, len(greeted))

    def held(buffer, side, at, length):
        if buffer >= window:
            return relay.at[pl.ds((buffer - window) * half + at, length)]
        return win[buffer].at[pl.ds(side * half + at, length)]

    def start(source, tree, k, hop):
        step, spot, buffer = hop
        at = (tree * chunks + k) * part
        pltpu.make_async_remote_copy(
            src_ref=source,
            dst_ref=held(buffer, h, at, part),
            send_sem=send.at[0],
            recv_sem=got.at[buffer, tree, k],
            device_id=there(step, spot),
            device_id_type=MESH,
        ).start()

    def passed(buffer, side, at, length):
        return pltpu.make_async_remote_copy(
            src_ref=held(buffer, side, at, length),
            dst_ref=held(buffer, side, at, length),
            send_sem=give.at[buffer],
            recv_sem=take.at[buffer],
            device_id=partner,
            device_id_type=MESH,
        )

    def places(emit):
        for spot in range(GROUP):

            @pl.when(q == spot)
            def _(spot=spot):
                emit(spot)

    def emit_own(spot):
        for tree, k, hop in own[spot]:
            at = (tree * chunks + k) * part
            start(density.at[h, pl.ds(at, part)], tree, k, hop)

    places(emit_own)

    mine = [
        pltpu.make_async_copy(density.at[r], win[0].at[pl.ds(r * slots, slots)], local.at[r])
        for r in range(rows)
    ]
    listed = pltpu.make_async_copy(tasks_in, tasks, local.at[rows])
    listed.start()
    for copy in mine:
        copy.start()
    for t in range(window):
        win[t][stored] = jnp.zeros((size, size), density.dtype)

    listed.wait()
    mine_slots = out.shape[1]
    entries = rows * mine_slots * rows
    entry = lax.broadcasted_iota(jnp.int32, (entries, count), 0)
    column = lax.broadcasted_iota(jnp.int32, (entries, count), 1)
    entry_row = entry // (mine_slots * rows)
    entry_slot = entry // rows % mine_slots
    entry_inner = entry % rows
    wanted = entry_row * slots + h * mine_slots + entry_slot
    found = jnp.zeros((entries, count), jnp.int32)
    for t in range(window):
        first = jnp.broadcast_to(tasks[0, 0, t : t + 1, :], (entries, count))
        second = jnp.broadcast_to(tasks[1, 0, t : t + 1, :], (entries, count))
        result = jnp.broadcast_to(tasks[2, 0, t : t + 1, :], (entries, count))
        inner_ok = second // slots == entry_inner
        hit = jnp.logical_and(inner_ok, result == wanted)
        spot = jnp.max(jnp.where(hit, second, -1), axis=1, keepdims=True)
        spot = jnp.where(spot < 0, stored, spot)
        hit_row = jnp.logical_and(inner_ok, result // slots == entry_row)
        line = jnp.max(jnp.where(hit_row, first, 0), axis=1, keepdims=True)
        found = jnp.where(column == t, spot, found)
        found = jnp.where(column == window + t, line, found)
    table[...] = found
    fetch = pltpu.make_async_copy(table, spots, local.at[rows])
    fetch.start()
    fetch.wait()
    for copy in mine:
        copy.wait()

    for r in range(rows):
        for t in range(window):
            for j in range(rows):
                spot = spots[r * mine_slots * rows + j, window + t]
                at = (t * rows + j) * size
                lines[r, :, at : at + size] = win[0][spot]

    pair = 2

    def multiply(offsets, begin, end):
        for t in offsets:
            if t > 0:
                passed(t, 1 - h, 0, half).wait_recv()
                passed(t, h, 0, half).wait_send()
        width = rows * size
        for r in range(rows):

            def step(m, _, r=r):
                columns = []
                for s in range(pair):
                    at = (r * mine_slots + m * pair + s) * rows
                    blocks = [win[t][spots[at + j, t]] for t in offsets for j in range(rows)]
                    columns.append(jnp.concatenate(blocks, axis=0))
                right = jnp.concatenate(columns, axis=1)
                left = jnp.concatenate([lines[r, :, t * width : (t + 1) * width] for t in offsets], axis=1)
                value = jnp.dot(left, right, preferred_element_type=jnp.float32)
                if not begin:
                    value = value + total[r, m]
                if not end:
                    total[r, m] = value
                    return 0
                for s in range(pair):
                    out[r, m * pair + s] = value[:, s * size : (s + 1) * size].astype(out.dtype)
                return 0

            lax.fori_loop(0, mine_slots // pair, step, 0, unroll=8)

    def emit_flow(spot):
        sent = len(own[spot])
        for _, buffer, event in events[spot]:
            if event is None:
                multiply([buffer], False, False)
                continue
            tree, k, onward = event
            at = (tree * chunks + k) * part
            chunk = held(buffer, h, at, part)
            pltpu.make_async_copy(chunk, chunk, got.at[buffer, tree, k]).wait()
            for hop in onward:
                start(chunk, tree, k, hop)
            sent += len(onward)
            if buffer < window:
                passed(buffer, h, at, part).start()
        multiply(tails[spot], False, True)
        left = sent * part
        while left > 0:
            length = min(left, half)
            chunk = held(window, h, 0, length)
            pltpu.make_async_copy(chunk, chunk, send.at[0]).wait()
            left -= length

    multiply([0], True, False)
    places(emit_flow)


def solution(mesh):
    n = mesh.shape["blk"]
    layers = mesh.shape["depth"]

    def body(density, product_tasks):
        rows, slots, size = density.shape[0], density.shape[1], density.shape[2]
        window, count = product_tasks.shape[2], product_tasks.shape[3]
        stored = rows * slots
        mine_slots = slots // layers
        entries = rows * mine_slots * rows
        chunks = 8
        trees = 2
        chunk_bytes = slots // (trees * chunks) * size * size * density.dtype.itemsize
        own, events, tails, total = make_plan(chunks, chunk_bytes)
        density = pltpu.with_memory_space_constraint(density, pltpu.HBM)
        product_tasks = pltpu.with_memory_space_constraint(product_tasks, pltpu.HBM)
        return pl.pallas_call(
            functools.partial(kernel, n, own, events, tails),
            out_shape=jax.ShapeDtypeStruct((rows, mine_slots, size, size), density.dtype),
            in_specs=[
                pl.BlockSpec(memory_space=pltpu.HBM),
                pl.BlockSpec(memory_space=pltpu.HBM),
            ],
            out_specs=pl.BlockSpec(memory_space=pltpu.VMEM),
            scratch_shapes=[
                *[pltpu.VMEM((stored + 1, size, size), density.dtype)] * window,
                pltpu.VMEM(((total - window) * slots, size, size), density.dtype),
                pltpu.VMEM((rows, size, window * rows * size), density.dtype),
                pltpu.VMEM((rows, mine_slots // 2, size, 2 * size), jnp.float32),
                pltpu.VMEM(product_tasks.shape, jnp.int32),
                pltpu.VMEM((entries, count), jnp.int32),
                pltpu.SMEM((entries, count), jnp.int32),
                pltpu.SemaphoreType.DMA((1,)),
                pltpu.SemaphoreType.DMA((total, trees, chunks)),
                pltpu.SemaphoreType.DMA((window,)),
                pltpu.SemaphoreType.DMA((window,)),
                pltpu.SemaphoreType.DMA((rows + 1,)),
            ],
            compiler_params=pltpu.CompilerParams(collective_id=0, has_side_effects=True, vmem_limit_bytes=24 << 20),
        )(density, product_tasks)

    placed = (P(("shift", "blk"), None, None, None), P(None, ("shift", "blk"), None, None))
    return jax.shard_map(
        body,
        mesh=mesh,
        in_specs=placed,
        out_specs=P(("shift", "blk"), "depth", None, None),
        check_vma=False,
    )
```
